32 devices in a mesh: head: 2 (over core), seq: 16 (over z, y, x).
Axes of the slice: x: 2, y: 2, z: 4, core: 2. Of those that a mesh axis runs over, the one named last changes fastest.
Arguments:
- queries: bfloat16 [8192, 5120], P(('seq', 'head')), may hold values from -8 to 8
- key_states: bfloat16 [8192, 5120], P(('seq', 'head')), may hold values from -8 to 8
- value_states: bfloat16 [8192, 5120], P(('seq', 'head')), may hold values from -6 to 6
- cluster_perm: int32 [40, 8192], P('head', 'seq'), may hold values from 0 to 8191, as said below
- block_mask: int32 [40, 64, 64], P('head', 'seq'), may hold values from 0 to 1, as said below
Outputs:
- attention_out: bfloat16 [8192, 5120], P(('seq', 'head'))
The draws below stay inside these ranges and needn't reach their ends.
Inputs may be any that keep to these rules, and one draw needn't show every extreme that they name: `cluster_perm`: for each head, positions k * 512 to (k + 1) * 512 - 1 list the tokens k * 512 to (k + 1) * 512 - 1, each once. `block_mask`: for each head and each aligned run of 4 query blocks, the key blocks used by some query block of the run number exactly 1. For such a run and the 20 heads g * 20 to (g + 1) * 20 - 1, the (head, key block) pairs so used that lie in one aligned run of 4 key blocks number at most 2, and exactly 2 in some run. Every query block uses 1 to 1 key blocks, and some query block of every run uses 1, for every head.
All inputs are finite; a program needn't handle non-finite values.
Results may differ from the reference program's by a relative error of at most 0.0049.
Values may be sent and summed in bfloat16 or wider, within the bound.
A program may use at most 128 MiB of HBM per device.

```python
import math
import jax
import jax.numpy as jnp
from jax import lax

HEADS = 40
HEAD_DIM = 128
BLOCK = 128
ROWS_SEQ = 512
TOKENS = 8192
BLOCKS = 64
PICKS = 1
LIVE = 1
CAP = 2
N_HEAD = 2
N_SEQ = 16


def draw_queries(key, part):
    gaussian = jax.random.truncated_normal(jax.random.fold_in(key, 11), -6.0, 6.0, (TOKENS, HEADS, HEAD_DIM), jnp.float32)
    return gaussian.reshape(TOKENS, HEADS * HEAD_DIM).astype(jnp.bfloat16)


def draw_key_states(key, part):
    gaussian = jax.random.truncated_normal(jax.random.fold_in(key, 21), -6.0, 6.0, (TOKENS, HEADS, HEAD_DIM), jnp.float32)
    return gaussian.reshape(TOKENS, HEADS * HEAD_DIM).astype(jnp.bfloat16)


def draw_cluster_perm(key, part):
    random_bits = jax.random.bits(jax.random.fold_in(key, 31), (HEADS, N_SEQ, ROWS_SEQ))
    local_order = jnp.argsort(random_bits, axis=-1, stable=True).astype(jnp.int32)
    offsets = (jnp.arange(N_SEQ, dtype=jnp.int32) * ROWS_SEQ)[None, :, None]
    return (local_order + offsets).reshape(HEADS, TOKENS)


def draw_block_mask(key, part):
    heads_group = HEADS // N_HEAD
    shard_blocks = ROWS_SEQ // BLOCK
    slot_count = N_SEQ * CAP
    filled_count = heads_group * PICKS
    slot_owner = jnp.arange(slot_count, dtype=jnp.int32) // CAP
    slot_index = jnp.arange(slot_count, dtype=jnp.int32) % CAP
    star_owner = jax.random.randint(jax.random.fold_in(key, 41), (N_HEAD, N_SEQ), 0, N_SEQ)
    jitter = jax.random.randint(jax.random.fold_in(key, 42), (N_HEAD, N_SEQ, slot_count), 0, 1 << 20)
    priority = jitter + jnp.where(slot_owner[None, None, :] == star_owner[:, :, None], 0, 1 << 21)
    ranking = jnp.argsort(priority, axis=-1, stable=True)
    position = jnp.argsort(ranking, axis=-1, stable=True).astype(jnp.int32)
    is_filled = (position < filled_count).astype(jnp.int32)
    head_local = position % heads_group
    rotate = jax.random.randint(jax.random.fold_in(key, 43), (N_HEAD, N_SEQ, N_SEQ * heads_group), 0, shard_blocks)
    rot_pick = jnp.take_along_axis(rotate, slot_owner[None, None, :] * heads_group + head_local, axis=-1)
    key_block = slot_owner[None, None, :] * shard_blocks + (slot_index[None, None, :] + rot_pick) % shard_blocks
    group_ids = jnp.arange(N_HEAD, dtype=jnp.int32)[:, None, None]
    shard_ids = jnp.arange(N_SEQ, dtype=jnp.int32)[None, :, None]
    needed = jnp.zeros((N_HEAD, N_SEQ, heads_group, BLOCKS), jnp.int32)
    needed = needed.at[group_ids, shard_ids, head_local, key_block].max(is_filled)
    prefix = (jnp.cumsum(needed, axis=-1) - needed).astype(jnp.int32)
    chosen = (needed[..., None] == 1) & (prefix[..., None] == jnp.arange(PICKS, dtype=jnp.int32))
    picked = jnp.sum(jnp.where(chosen, jnp.arange(BLOCKS, dtype=jnp.int32)[:, None], 0), axis=-2).astype(jnp.int32)
    pick_ids = jnp.arange(PICKS, dtype=jnp.int32)
    query_ids = jnp.arange(shard_blocks, dtype=jnp.int32)
    home_bits = pick_ids[None, :] % shard_blocks == query_ids[:, None]
    home_count = jnp.sum(home_bits, axis=1).astype(jnp.int32)
    target = jax.random.randint(jax.random.fold_in(key, 44), (N_HEAD, N_SEQ, heads_group, shard_blocks), 1, LIVE + 1)
    star_query = jax.random.randint(jax.random.fold_in(key, 45), (N_HEAD, N_SEQ, heads_group), 0, shard_blocks)
    target = jnp.where(query_ids == star_query[..., None], LIVE, target)
    target = jnp.maximum(target, home_count)
    draw_scores = jax.random.randint(jax.random.fold_in(key, 46), (N_HEAD, N_SEQ, heads_group, shard_blocks, PICKS), 0, 1 << 20)
    draw_scores = jnp.where(home_bits, 1 << 21, draw_scores)
    extra_rank = jnp.argsort(jnp.argsort(draw_scores, axis=-1, stable=True), axis=-1, stable=True).astype(jnp.int32)
    live_bits = (home_bits | (extra_rank < (target - home_count)[..., None])).astype(jnp.int32)
    mask_grid = jnp.zeros((N_HEAD, N_SEQ, heads_group, shard_blocks, BLOCKS), jnp.int32)
    mask_grid = mask_grid.at[jnp.arange(N_HEAD)[:, None, None, None, None], jnp.arange(N_SEQ)[None, :, None, None, None], jnp.arange(heads_group)[None, None, :, None, None], query_ids[None, None, None, :, None], picked[:, :, :, None, :]].max(live_bits)
    return mask_grid.transpose(0, 2, 1, 3, 4).reshape(HEADS, BLOCKS, BLOCKS)


def level_of(stream_key, shape, cuts, low, high):
    def one(dim, shards_of):
        draws = jax.random.uniform(jax.random.fold_in(jax.random.fold_in(stream_key, 6), dim), (shards_of,), jnp.float32, low / len(cuts), high / len(cuts))
        return jnp.repeat(jnp.exp(draws), shape[dim] // shards_of).reshape((-1,) + (1,) * (len(shape) - dim - 1))

    gain = one(*cuts[0])
    for cut in cuts[1:]:
        gain = gain * one(*cut)
    return gain


def scatter_about(stream_key, shape, deviation, bound, split=(), kind=jnp.bfloat16):
    gain = level_of(stream_key, shape, split, -0.22, 0.18) if split else 1.0
    array = jax.random.normal(stream_key, shape, jnp.float32) * deviation * gain
    return jnp.minimum(jnp.maximum(array, -bound), bound).astype(kind)


def setup_inputs(seed: int = 0) -> dict:
    seeds = jax.random.split(jax.random.key(seed), 6)
    return {
        "queries": draw_queries(jax.random.fold_in(seeds[5], 71), 0),
        "key_states": draw_key_states(jax.random.fold_in(seeds[5], 71), 0),
        "value_states": scatter_about(seeds[2], (TOKENS, HEADS * HEAD_DIM), 1.0, 6.0, ((0, 32),)),
        "cluster_perm": draw_cluster_perm(jax.random.fold_in(seeds[5], 71), 0),
        "block_mask": draw_block_mask(jax.random.fold_in(seeds[5], 71), 0),
    }


def reference(queries, key_states, value_states, cluster_perm, block_mask):

    def cluster_order(flat_rows):
        grid_view = flat_rows.reshape(TOKENS, HEADS, HEAD_DIM).transpose(1, 0, 2)
        return jnp.take_along_axis(grid_view, cluster_perm[:, :, None].astype(jnp.int32), axis=1)
    query_sorted = cluster_order(queries)
    key_sorted = cluster_order(key_states)
    value_sorted = cluster_order(value_states)
    score_scale = 1.0 / math.sqrt(HEAD_DIM)
    slot_ids = jnp.arange(LIVE, dtype=jnp.int32)
    block_ids = jnp.arange(BLOCKS, dtype=jnp.int32)

    def one_head(operands):
        query_head, key_head, value_head, mask_head = operands
        prefix = (jnp.cumsum(mask_head, axis=1) - mask_head).astype(jnp.int32)
        chosen = (mask_head[:, :, None] == 1) & (prefix[:, :, None] == slot_ids[None, None, :])
        which_block = lax.optimization_barrier(jnp.sum(jnp.where(chosen, block_ids[None, :, None], 0), axis=1)).astype(jnp.int32)
        usable = jnp.any(chosen, axis=1)
        key_sel = jnp.take(key_head.reshape(BLOCKS, BLOCK, HEAD_DIM), which_block, axis=0)
        value_sel = jnp.take(value_head.reshape(BLOCKS, BLOCK, HEAD_DIM), which_block, axis=0)
        query_blocks = query_head.reshape(BLOCKS, BLOCK, HEAD_DIM).astype(jnp.float32)
        scores = jnp.einsum('nid,nljd->nilj', query_blocks, key_sel.astype(jnp.float32), precision=lax.Precision.HIGHEST) * score_scale
        scores = jnp.where(usable[:, None, :, None], scores, -jnp.inf)
        row_top = lax.optimization_barrier(jnp.max(scores, axis=(2, 3), keepdims=True))
        exponent = jnp.exp(scores - row_top)
        row_total = lax.optimization_barrier(jnp.sum(exponent, axis=(2, 3), keepdims=True))
        weights = (exponent / row_total).astype(jnp.bfloat16)
        attended = jnp.einsum('nilj,nljd->nid', weights.astype(jnp.float32), value_sel.astype(jnp.float32), precision=lax.Precision.HIGHEST)
        return attended.astype(jnp.bfloat16).reshape(TOKENS, HEAD_DIM)
    attended = lax.map(one_head, (query_sorted, key_sorted, value_sorted, block_mask))
    restored = jnp.zeros((HEADS, TOKENS, HEAD_DIM), jnp.bfloat16)
    restored = restored.at[jnp.arange(HEADS, dtype=jnp.int32)[:, None], cluster_perm.astype(jnp.int32)].set(attended)
    return restored.transpose(1, 0, 2).reshape(TOKENS, HEADS * HEAD_DIM)
```

```python
import functools
import math

import jax
import jax.numpy as jnp
from jax import lax
from jax.experimental import pallas as pl
from jax.experimental.pallas import tpu as pltpu
from jax.sharding import PartitionSpec as P

HEAD_DIM = 128
BLOCK = 128
MESH = pl.DeviceIdType.MESH
HIGHEST = lax.Precision.HIGHEST


def iota(shape, dim):
    return lax.broadcasted_iota(jnp.int32, shape, dim)


def partner_of(me, step, count):
    if count & (count - 1):
        raise ValueError("seq size")
    peer = 0
    bit = 1
    while bit < count:
        peer = peer + bit * (((me // bit) + (step // bit)) % 2)
        bit *= 2
    return peer


def routing_kernel(shard_blocks, capacity, picks, mask_ref, req_ref, pos_ref):
    heads, _, blocks = mask_ref.shape
    seq_count = blocks // shard_blocks
    needed = jnp.max(mask_ref[...], axis=1).astype(jnp.float32)
    row, col = iota((blocks, blocks), 0), iota((blocks, blocks), 1)
    same = (row // shard_blocks) == (col // shard_blocks)
    dot = functools.partial(jnp.dot, precision=HIGHEST, preferred_element_type=jnp.float32)
    ones = lambda flag: flag.astype(jnp.float32)
    by_owner = dot(needed, ones(same))
    before_in_owner = dot(needed, ones(same & (row < col)))
    before_all = dot(needed, ones(row < col))
    lower = ones(iota((heads, heads), 1) < iota((heads, heads), 0))
    rank = dot(lower, by_owner) + before_in_owner
    head_ids, block_ids = iota((heads, blocks), 0), iota((heads, blocks), 1)
    pair = (head_ids * shard_blocks + block_ids % shard_blocks).astype(jnp.float32)
    slot_row = iota((128, blocks), 0)
    sums = jnp.zeros((128, blocks), jnp.float32)
    for c in range(capacity):
        hit = jnp.where((rank == c) & (needed > 0.5), pair, 0.0)
        sums = jnp.where(slot_row == c, jnp.sum(hit, axis=0, keepdims=True), sums)
    owner_t = ones(iota((seq_count, blocks), 1) // shard_blocks == iota((seq_count, blocks), 0))
    asked = lax.dot_general(
        owner_t, sums, (((1,), (1,)), ((), ())), precision=HIGHEST,
        preferred_element_type=jnp.float32,
    )
    req_ref[...] = (asked + 0.5).astype(jnp.int32)[:, None, :]
    position = (block_ids // shard_blocks * capacity).astype(jnp.float32) + rank
    lane = iota((heads, 128), 1)
    table = jnp.zeros((heads, 128), jnp.float32)
    for p in range(picks):
        here = jnp.where((before_all == p) & (needed > 0.5), position, 0.0)
        table = jnp.where(lane == p, jnp.sum(here, axis=1, keepdims=True), table)
    pos_ref[...] = (table + 0.5).astype(jnp.int32)


def swap_kernel(
    seq_count, pieces, key_ref, value_ref, req_ref, pos_ref,
    key_out, value_out, asked_ref, pos_out, sends, recvs, req_send, req_recv, pos_sem,
):
    group, me = lax.axis_index("head"), lax.axis_index("seq")
    other = 1 - group
    barrier = pltpu.get_barrier_semaphore()
    pl.semaphore_signal(barrier, inc=1, device_id={"head": other}, device_id_type=MESH)

    def greet(step, carry):
        pl.semaphore_signal(
            barrier, inc=1, device_id={"seq": partner_of(me, step, seq_count)}, device_id_type=MESH
        )
        return carry

    lax.fori_loop(1, seq_count, greet, 0)
    pl.semaphore_wait(barrier, seq_count)

    def ask(step):
        peer = partner_of(me, step, seq_count)
        return pltpu.make_async_remote_copy(
            src_ref=req_ref.at[peer], dst_ref=asked_ref.at[me],
            send_sem=req_send.at[step], recv_sem=req_recv.at[step],
            device_id={"seq": peer}, device_id_type=MESH,
        )

    def start(step, carry):
        ask(step).start()
        return carry

    lax.fori_loop(1, seq_count, start, 0)
    tell = pltpu.make_async_remote_copy(
        src_ref=pos_ref, dst_ref=pos_out, send_sem=pos_sem.at[0], recv_sem=pos_sem.at[1],
        device_id={"head": other}, device_id_type=MESH,
    )
    tell.start()
    rows, half = key_out.shape
    step_rows = rows // pieces
    columns = pl.ds(pl.multiple_of(other * half, 128), half)
    swaps = []
    for number, (src, dst) in enumerate(((key_ref, key_out), (value_ref, value_out))):
        for piece in range(pieces):
            part = pl.ds(piece * step_rows, step_rows)
            at = number * pieces + piece
            swaps.append(
                pltpu.make_async_remote_copy(
                    src_ref=src.at[part, columns], dst_ref=dst.at[part],
                    send_sem=sends.at[at], recv_sem=recvs.at[at],
                    device_id={"head": other}, device_id_type=MESH,
                )
            )
    for copy in swaps:
        copy.start()
    asked_ref[me] = req_ref[me]

    def finish(step, carry):
        peer = partner_of(me, step, seq_count)
        copy = pltpu.make_async_remote_copy(
            src_ref=req_ref.at[peer], dst_ref=asked_ref.at[peer],
            send_sem=req_send.at[step], recv_sem=req_recv.at[step],
            device_id={"seq": peer}, device_id_type=MESH,
        )
        copy.wait()
        return carry

    lax.fori_loop(1, seq_count, finish, 0)
    tell.wait()
    for copy in swaps:
        copy.wait()


def gather_kernel(
    shard_blocks, capacity, ids, asked, perm_ref, key_own, value_own, key_far, value_far,
    out_ref, rows_ref,
):
    group, me = ids[0], ids[1]
    step = pl.program_id(0)
    count = out_ref.shape[0]
    rows = key_own.shape[0]
    base = me * (2 * rows)
    wanted = []
    for i in range(count):
        for c in range(capacity):
            pair = asked[step * count + i, 0, c]
            head, block = pair // shard_blocks, pair % shard_blocks
            wanted.append((i, c, head))
            places = perm_ref[pl.ds(head, 1), :]
            chosen = places[:, :BLOCK]
            for b in range(1, shard_blocks):
                chosen = jnp.where(block == b, places[:, b * BLOCK : (b + 1) * BLOCK], chosen)
            rows_ref[i * capacity + c : i * capacity + c + 1, :] = chosen
    turned = rows_ref[...].T
    token = iota((BLOCK, rows), 1)
    near = token + (base + group * rows)
    far = token + (base + (1 - group) * rows)
    for i, c, head in wanted:
        at = i * capacity + c
        column = turned[:, at : at + 1]
        near_table = (column == near).astype(jnp.float32).astype(jnp.bfloat16)
        far_table = (column == far).astype(jnp.float32).astype(jnp.bfloat16)
        columns = pl.ds(pl.multiple_of(head * HEAD_DIM, HEAD_DIM), HEAD_DIM)
        for which, (own, away) in enumerate(((key_own, key_far), (value_own, value_far))):
            got = jnp.dot(near_table, own[:, columns], preferred_element_type=jnp.float32)
            got += jnp.dot(far_table, away[:, columns], preferred_element_type=jnp.float32)
            out_ref[i, c, :, which * HEAD_DIM : (which + 1) * HEAD_DIM] = got.astype(jnp.bfloat16)


def exchange_kernel(seq_count, send_ref, got_ref, sends, recvs, relay_send, relay_recv, own_sem):
    group, me = lax.axis_index("head"), lax.axis_index("seq")
    other = 1 - group
    barrier = pltpu.get_barrier_semaphore()
    pl.semaphore_signal(barrier, inc=1, device_id={"head": other}, device_id_type=MESH)

    def greet(step, carry):
        pl.semaphore_signal(
            barrier, inc=1, device_id={"seq": partner_of(me, step, seq_count)}, device_id_type=MESH
        )
        return carry

    lax.fori_loop(1, seq_count, greet, 0)
    pl.semaphore_wait(barrier, seq_count)

    def deliver(step, landing):
        peer = partner_of(me, step, seq_count)
        return pltpu.make_async_remote_copy(
            src_ref=send_ref.at[peer], dst_ref=got_ref.at[0, peer if landing else me],
            send_sem=sends.at[step], recv_sem=recvs.at[step],
            device_id={"seq": peer}, device_id_type=MESH,
        )

    def relay(step):
        peer = partner_of(me, step, seq_count)
        return pltpu.make_async_remote_copy(
            src_ref=got_ref.at[0, peer], dst_ref=got_ref.at[1, peer],
            send_sem=relay_send.at[step], recv_sem=relay_recv.at[step],
            device_id={"head": other}, device_id_type=MESH,
        )

    def start(i, carry):
        deliver(seq_count - 1 - i, False).start()
        return carry

    lax.fori_loop(0, seq_count - 1, start, 0)
    mine = pltpu.make_async_copy(send_ref.at[me], got_ref.at[0, me], own_sem)
    mine.start()
    share = pltpu.make_async_remote_copy(
        src_ref=send_ref.at[me], dst_ref=got_ref.at[1, me],
        send_sem=relay_send.at[0], recv_sem=relay_recv.at[0],
        device_id={"head": other}, device_id_type=MESH,
    )
    share.start()

    def pass_on(i, carry):
        step = seq_count - 1 - i
        deliver(step, True).wait_recv()
        relay(step).start()
        return carry

    lax.fori_loop(0, seq_count - 1, pass_on, 0)

    def finish(step, carry):
        deliver(step, True).wait_send()
        relay(step).wait()
        return carry

    lax.fori_loop(1, seq_count, finish, 0)
    mine.wait()
    share.wait()


def attend_kernel(heads, picks, slots, masked, ids, pos_own, pos_far, *refs):
    if masked:
        query_ref, kv_ref, allow_ref, out_ref = refs
    else:
        query_ref, kv_ref, out_ref = refs
    group = ids[0]
    width = query_ref.shape[1] // HEAD_DIM
    scale = 1.0 / math.sqrt(HEAD_DIM)
    for w in range(width):
        head = pl.program_id(0) * width + w
        away = (head // heads) != group
        local = head % heads
        columns = slice(w * HEAD_DIM, (w + 1) * HEAD_DIM)
        query = query_ref[:, columns]
        scores, values = [], []
        for p in range(picks):
            slot = jnp.where(away, pos_far[local, p] + slots, pos_own[local, p])
            key = kv_ref[slot, :, :HEAD_DIM]
            values.append(kv_ref[slot, :, HEAD_DIM:])
            score = lax.dot_general(
                query, key, (((1,), (1,)), ((), ())), preferred_element_type=jnp.float32
            ) * scale
            if masked:
                score = jnp.where(allow_ref[w, :, p : p + 1] > 0, score, -jnp.inf)
            scores.append(score)
        top = jnp.max(scores[0], axis=1, keepdims=True)
        for score in scores[1:]:
            top = jnp.maximum(top, jnp.max(score, axis=1, keepdims=True))
        exps = [jnp.exp(score - top) for score in scores]
        total = jnp.sum(exps[0], axis=1, keepdims=True)
        for e in exps[1:]:
            total = total + jnp.sum(e, axis=1, keepdims=True)
        inverse = 1.0 / total
        mixed = None
        for e, value in zip(exps, values):
            part = jnp.dot(
                (e * inverse).astype(jnp.bfloat16), value, preferred_element_type=jnp.float32
            )
            mixed = part if mixed is None else mixed + part
        out_ref[:, columns] = mixed.astype(jnp.bfloat16)


def token_allow(cluster_perm, block_mask, picks, me, shard_rows):
    needed = jnp.max(block_mask, axis=1)
    prefix = jnp.cumsum(needed, axis=1) - needed
    chosen = (needed[:, :, None] == 1) & (prefix[:, :, None] == jnp.arange(picks)[None, None, :])
    live = jnp.einsum(
        "hqb,hbp->hqp", block_mask.astype(jnp.float32), chosen.astype(jnp.float32)
    )
    group_heads = cluster_perm.shape[0]
    local = cluster_perm - me * shard_rows
    place = jnp.zeros((group_heads, shard_rows), jnp.int32)
    place = place.at[jnp.arange(group_heads)[:, None], local].set(
        jnp.broadcast_to(jnp.arange(shard_rows, dtype=jnp.int32) // BLOCK, local.shape)
    )
    by_token = jnp.take_along_axis(live, place[:, :, None], axis=1).astype(jnp.float32)
    return lax.all_to_all(by_token, "head", split_axis=1, concat_axis=0, tiled=True)


def shards(queries, key_states, value_states, cluster_perm, block_mask):
    group_heads, shard_rows = cluster_perm.shape
    shard_blocks = shard_rows // BLOCK
    seq_count = lax.axis_size("seq")
    block_total = block_mask.shape[2]
    picks = max(1, block_total // 64)
    capacity = max(
        1, min(shard_blocks, (group_heads * picks * 8 + 5 * seq_count - 1) // (5 * seq_count))
    )
    slots = seq_count * capacity
    rows, columns = queries.shape
    half = columns // 2
    group, me = lax.axis_index("head"), lax.axis_index("seq")
    ids = jnp.stack([group, me]).astype(jnp.int32)
    vmem = pl.BlockSpec(memory_space=pltpu.VMEM)
    smem = pl.BlockSpec(memory_space=pltpu.SMEM)
    anywhere = pl.BlockSpec(memory_space=pl.ANY)
    struct = jax.ShapeDtypeStruct
    bf16, i32 = jnp.bfloat16, jnp.int32

    requests, positions = pl.pallas_call(
        functools.partial(routing_kernel, shard_blocks, capacity, picks),
        out_shape=(struct((seq_count, 1, 128), i32), struct((group_heads, 128), i32)),
        in_specs=[vmem], out_specs=(vmem, vmem), name="routing",
    )(block_mask)

    pieces = 4
    dma = pltpu.SemaphoreType.DMA
    key_far, value_far, asked, pos_far = pl.pallas_call(
        functools.partial(swap_kernel, seq_count, pieces),
        out_shape=(
            struct((rows, half), bf16), struct((rows, half), bf16),
            struct((seq_count, 1, 128), i32), struct((group_heads, 128), i32),
        ),
        in_specs=[anywhere, anywhere, vmem, vmem],
        out_specs=(anywhere, anywhere, vmem, vmem),
        scratch_shapes=[
            dma((2 * pieces,)), dma((2 * pieces,)), dma((seq_count,)), dma((seq_count,)), dma((2,)),
        ],
        compiler_params=pltpu.CompilerParams(collective_id=0, has_side_effects=True),
        name="swap",
    )(key_states, value_states, requests, positions)

    steps = 4 if seq_count % 4 == 0 else 1
    share = seq_count // steps
    own_half = pl.BlockSpec((rows, half), lambda i, ids, asked: (0, ids[0]))
    whole_half = pl.BlockSpec((rows, half), lambda i, ids, asked: (0, 0))
    to_send = pl.pallas_call(
        functools.partial(gather_kernel, shard_blocks, capacity),
        out_shape=struct((seq_count, capacity, BLOCK, 2 * HEAD_DIM), bf16),
        grid_spec=pltpu.PrefetchScalarGridSpec(
            num_scalar_prefetch=2,
            grid=(steps,),
            in_specs=[
                pl.BlockSpec((group_heads, shard_rows), lambda i, ids, asked: (0, 0)),
                own_half, own_half, whole_half, whole_half,
            ],
            out_specs=pl.BlockSpec(
                (share, capacity, BLOCK, 2 * HEAD_DIM), lambda i, ids, asked: (i, 0, 0, 0)
            ),
            scratch_shapes=[pltpu.VMEM((128, 128), i32)],
        ),
        name="gather",
    )(ids, asked, cluster_perm, key_states, value_states, key_far, value_far)

    got = pl.pallas_call(
        functools.partial(exchange_kernel, seq_count),
        out_shape=struct((2, seq_count, capacity, BLOCK, 2 * HEAD_DIM), bf16),
        in_specs=[anywhere], out_specs=anywhere,
        scratch_shapes=[dma((seq_count,)) for _ in range(4)] + [dma],
        compiler_params=pltpu.CompilerParams(collective_id=1, has_side_effects=True),
        name="exchange",
    )(to_send)
    got = got.reshape(2 * slots, BLOCK, 2 * HEAD_DIM)

    masked = picks > 1
    total_heads = columns // HEAD_DIM
    width = 8 if total_heads % 8 == 0 else 1
    in_specs = [
        pl.BlockSpec((rows, width * HEAD_DIM), lambda i, *_: (0, i)),
        pl.BlockSpec(got.shape, lambda i, *_: (0, 0, 0)),
    ]
    operands = [queries, got]
    if masked:
        in_specs.append(pl.BlockSpec((width, rows, picks), lambda i, *_: (i, 0, 0)))
        operands.append(token_allow(cluster_perm, block_mask, picks, me, shard_rows))
    return pl.pallas_call(
        functools.partial(attend_kernel, group_heads, picks, slots, masked),
        out_shape=struct((rows, columns), bf16),
        grid_spec=pltpu.PrefetchScalarGridSpec(
            num_scalar_prefetch=3,
            grid=(total_heads // width,),
            in_specs=in_specs,
            out_specs=pl.BlockSpec((rows, width * HEAD_DIM), lambda i, *_: (0, i)),
        ),
        compiler_params=pltpu.CompilerParams(vmem_limit_bytes=56 * 1024 * 1024),
        name="attend",
    )(ids, positions, pos_far, *operands)


def solution(mesh):
    rows = P(("seq", "head"), None)
    placed = (rows, rows, rows, P("head", "seq"), P("head", "seq", None))
    return jax.shard_map(shards, mesh=mesh, in_specs=placed, out_specs=rows, check_vma=False)
```

```python
import functools
import math

import jax
import jax.numpy as jnp
from jax import lax
from jax.experimental import pallas as pl
from jax.experimental.pallas import tpu as pltpu
from jax.sharding import PartitionSpec as P

HEAD_DIM = 128
BLOCK = 128
MESH = pl.DeviceIdType.MESH
HIGHEST = lax.Precision.HIGHEST


def iota(shape, dim):
    return lax.broadcasted_iota(jnp.int32, shape, dim)


def partner_of(me, step, count):
    if count & (count - 1):
        raise ValueError("seq size")
    peer = 0
    bit = 1
    while bit < count:
        peer = peer + bit * (((me // bit) + (step // bit)) % 2)
        bit *= 2
    return peer


def routing_kernel(shard_blocks, capacity, picks, mask_ref, req_ref, pos_ref):
    heads, _, blocks = mask_ref.shape
    seq_count = blocks // shard_blocks
    needed = jnp.max(mask_ref[...], axis=1).astype(jnp.float32)
    row, col = iota((blocks, blocks), 0), iota((blocks, blocks), 1)
    same = (row // shard_blocks) == (col // shard_blocks)
    dot = functools.partial(jnp.dot, precision=HIGHEST, preferred_element_type=jnp.float32)
    ones = lambda flag: flag.astype(jnp.float32)
    by_owner = dot(needed, ones(same))
    before_in_owner = dot(needed, ones(same & (row < col)))
    before_all = dot(needed, ones(row < col))
    lower = ones(iota((heads, heads), 1) < iota((heads, heads), 0))
    rank = dot(lower, by_owner) + before_in_owner
    head_ids, block_ids = iota((heads, blocks), 0), iota((heads, blocks), 1)
    pair = (head_ids * shard_blocks + block_ids % shard_blocks).astype(jnp.float32)
    slot_row = iota((128, blocks), 0)
    sums = jnp.zeros((128, blocks), jnp.float32)
    for c in range(capacity):
        hit = jnp.where((rank == c) & (needed > 0.5), pair, 0.0)
        sums = jnp.where(slot_row == 2 * c, jnp.sum(hit, axis=0, keepdims=True), sums)
        hit = jnp.where((rank == c) & (needed > 0.5), head_ids.astype(jnp.float32), 0.0)
        sums = jnp.where(slot_row == 2 * c + 1, jnp.sum(hit, axis=0, keepdims=True), sums)
    owner_t = ones(iota((seq_count, blocks), 1) // shard_blocks == iota((seq_count, blocks), 0))
    asked = lax.dot_general(
        owner_t, sums, (((1,), (1,)), ((), ())), precision=HIGHEST,
        preferred_element_type=jnp.float32,
    )
    req_ref[...] = (asked + 0.5).astype(jnp.int32)[:, None, :]
    position = (block_ids // shard_blocks * capacity).astype(jnp.float32) + rank
    lane = iota((heads, 128), 1)
    table = jnp.zeros((heads, 128), jnp.float32)
    for p in range(picks):
        here = jnp.where((before_all == p) & (needed > 0.5), position, 0.0)
        table = jnp.where(lane == p, jnp.sum(here, axis=1, keepdims=True), table)
    pos_ref[...] = (table + 0.5).astype(jnp.int32)


def order(i, me, count):
    top, next_bit = (me // (count // 2)) % 2, (me // (count // 4)) % 2
    end = (top + next_bit + 1) % 2
    return end * (1 + (i + count // 4 - 1) % (count - 1)) + (1 - end) * (count - 1 - i)


def exchange_kernel(
    seq_count, capacity,
    key_ref, value_ref, perm_ref, req_ref, pos_ref, got_ref, pos_out,
    near_kv, far_kv, asked_ref, asked, send_ref, rows_ref,
    load_sem, swap_send, swap_recv, req_send, req_recv, misc_sem,
    sends, recvs, relay_send, relay_recv,
):
    group, me = lax.axis_index("head"), lax.axis_index("seq")
    other = 1 - group
    heads, rows = near_kv.shape[1:3]
    barrier = pltpu.get_barrier_semaphore()
    pl.semaphore_signal(barrier, inc=1, device_id={"head": other}, device_id_type=MESH)

    def greet(step, carry):
        pl.semaphore_signal(
            barrier, inc=1, device_id={"seq": partner_of(me, step, seq_count)}, device_id_type=MESH
        )
        return carry

    lax.fori_loop(1, seq_count, greet, 0)
    loads = []
    for number, src in enumerate((key_ref, value_ref)):
        for head in range(heads):
            start_at = pl.multiple_of((group * heads + head) * HEAD_DIM, HEAD_DIM)
            loads.append(
                pltpu.make_async_copy(
                    src.at[:, pl.ds(start_at, HEAD_DIM)], near_kv.at[number, head],
                    load_sem.at[number * heads + head],
                )
            )
    for copy in loads:
        copy.start()
    pl.semaphore_wait(barrier, seq_count)

    def ask(step, landing):
        peer = partner_of(me, step, seq_count)
        return pltpu.make_async_remote_copy(
            src_ref=req_ref.at[peer], dst_ref=asked_ref.at[peer if landing else me],
            send_sem=req_send.at[step], recv_sem=req_recv.at[step],
            device_id={"seq": peer}, device_id_type=MESH,
        )

    def start_ask(step, carry):
        ask(step, False).start()
        return carry

    lax.fori_loop(1, seq_count, start_ask, 0)
    swaps = []
    for number, src in enumerate((key_ref, value_ref)):
        for head in range(heads):
            start_at = pl.multiple_of((other * heads + head) * HEAD_DIM, HEAD_DIM)
            at = number * heads + head
            swaps.append(
                pltpu.make_async_remote_copy(
                    src_ref=src.at[:, pl.ds(start_at, HEAD_DIM)], dst_ref=far_kv.at[number, head],
                    send_sem=swap_send.at[at], recv_sem=swap_recv.at[at],
                    device_id={"head": other}, device_id_type=MESH,
                )
            )
    for copy in swaps:
        copy.start()
    tell = pltpu.make_async_remote_copy(
        src_ref=pos_ref, dst_ref=pos_out, send_sem=misc_sem.at[0], recv_sem=misc_sem.at[1],
        device_id={"head": other}, device_id_type=MESH,
    )
    tell.start()
    keep = pltpu.make_async_copy(req_ref.at[me], asked_ref.at[me], misc_sem.at[2])
    keep.start()
    keep.wait()

    def finish_ask(step, carry):
        ask(step, True).wait()
        return carry

    lax.fori_loop(1, seq_count, finish_ask, 0)
    to_scalar = pltpu.make_async_copy(asked_ref, asked, misc_sem.at[3])
    to_scalar.start()
    to_scalar.wait()
    for copy in loads:
        copy.wait()
    for copy in swaps:
        copy.wait()

    base = me * (2 * rows)
    token = iota((BLOCK, rows), 1)
    near = token + (base + group * rows)
    far = token + (base + other * rows)
    rows_ref[...] = jnp.zeros_like(rows_ref)

    def gather(peer):
        chosen = []
        for c in range(capacity):
            rows_ref[c : c + 1, :] = perm_ref[asked[peer, 0, 2 * c]]
            chosen.append(asked[peer, 0, 2 * c + 1])
        turned = rows_ref[...].T
        for c, head in enumerate(chosen):
            column = turned[:, c : c + 1]
            near_table = (column == near).astype(jnp.float32).astype(jnp.bfloat16)
            far_table = (column == far).astype(jnp.float32).astype(jnp.bfloat16)
            for which in range(2):
                got = jnp.dot(near_table, near_kv[which, head], preferred_element_type=jnp.float32)
                got += jnp.dot(far_table, far_kv[which, head], preferred_element_type=jnp.float32)
                send_ref[peer, c, :, which * HEAD_DIM : (which + 1) * HEAD_DIM] = got.astype(
                    jnp.bfloat16
                )

    def deliver(step, landing):
        peer = partner_of(me, step, seq_count)
        return pltpu.make_async_remote_copy(
            src_ref=send_ref.at[peer], dst_ref=got_ref.at[0, peer if landing else me],
            send_sem=sends.at[step], recv_sem=recvs.at[step],
            device_id={"seq": peer}, device_id_type=MESH,
        )

    def relay(step):
        peer = partner_of(me, step, seq_count)
        return pltpu.make_async_remote_copy(
            src_ref=got_ref.at[0, peer], dst_ref=got_ref.at[1, peer],
            send_sem=relay_send.at[step], recv_sem=relay_recv.at[step],
            device_id={"head": other}, device_id_type=MESH,
        )

    gather(partner_of(me, order(0, me, seq_count), seq_count))

    def produce(i, carry):
        gather(partner_of(me, order(i, me, seq_count), seq_count))
        deliver(order(i - 1, me, seq_count), False).start()
        return carry

    lax.fori_loop(1, seq_count - 1, produce, 0)
    gather(me)
    deliver(order(seq_count - 2, me, seq_count), False).start()

    def pass_on(i, carry):
        step = order(i, me, seq_count)
        deliver(step, True).wait_recv()
        relay(step).start()
        return carry

    pass_on(0, 0)
    mine = pltpu.make_async_copy(send_ref.at[me], got_ref.at[0, me], misc_sem.at[4])
    mine.start()
    share = pltpu.make_async_remote_copy(
        src_ref=send_ref.at[me], dst_ref=got_ref.at[1, me],
        send_sem=relay_send.at[0], recv_sem=relay_recv.at[0],
        device_id={"head": other}, device_id_type=MESH,
    )
    share.start()
    lax.fori_loop(1, seq_count - 1, pass_on, 0)

    def finish(step, carry):
        deliver(step, True).wait_send()
        relay(step).wait()
        return carry

    lax.fori_loop(1, seq_count, finish, 0)
    mine.wait()
    share.wait()
    tell.wait()


def attend_kernel(heads, picks, slots, masked, ids, pos_own, pos_far, *refs):
    if masked:
        query_ref, kv_ref, allow_ref, out_ref = refs
    else:
        query_ref, kv_ref, out_ref = refs
    group = ids[0]
    width = query_ref.shape[1] // HEAD_DIM
    scale = 1.0 / math.sqrt(HEAD_DIM)
    slot_of, scores = [], []
    for w in range(width):
        head = pl.program_id(0) * width + w
        away = (head // heads) != group
        local = head % heads
        query = query_ref[:, w * HEAD_DIM : (w + 1) * HEAD_DIM]
        for p in range(picks):
            slot = jnp.where(away, pos_far[local, p] + slots, pos_own[local, p])
            slot_of.append(slot)
            score = lax.dot_general(
                query, kv_ref[slot, :, :HEAD_DIM], (((1,), (1,)), ((), ())),
                preferred_element_type=jnp.float32,
            ) * scale
            if masked:
                score = jnp.where(allow_ref[w, :, p : p + 1] > 0, score, -jnp.inf)
            scores.append(score)
    weights = []
    for w in range(width):
        own = scores[w * picks : (w + 1) * picks]
        top = functools.reduce(jnp.maximum, [jnp.max(s, axis=1, keepdims=True) for s in own])
        exps = [jnp.exp(s - top) for s in own]
        total = functools.reduce(jnp.add, [jnp.sum(e, axis=1, keepdims=True) for e in exps])
        inverse = 1.0 / total
        weights.extend([(e * inverse).astype(jnp.bfloat16) for e in exps])
    mixed = []
    for w in range(width):
        parts = [
            jnp.dot(
                weights[w * picks + p], kv_ref[slot_of[w * picks + p], :, HEAD_DIM:],
                preferred_element_type=jnp.float32,
            )
            for p in range(picks)
        ]
        mixed.append(functools.reduce(jnp.add, parts).astype(jnp.bfloat16))
    for w in range(width):
        out_ref[:, w * HEAD_DIM : (w + 1) * HEAD_DIM] = mixed[w]


def token_allow(cluster_perm, block_mask, picks, me, shard_rows):
    needed = jnp.max(block_mask, axis=1)
    prefix = jnp.cumsum(needed, axis=1) - needed
    chosen = (needed[:, :, None] == 1) & (prefix[:, :, None] == jnp.arange(picks)[None, None, :])
    live = jnp.einsum(
        "hqb,hbp->hqp", block_mask.astype(jnp.float32), chosen.astype(jnp.float32)
    )
    group_heads = cluster_perm.shape[0]
    local = cluster_perm - me * shard_rows
    place = jnp.zeros((group_heads, shard_rows), jnp.int32)
    place = place.at[jnp.arange(group_heads)[:, None], local].set(
        jnp.broadcast_to(jnp.arange(shard_rows, dtype=jnp.int32) // BLOCK, local.shape)
    )
    by_token = jnp.take_along_axis(live, place[:, :, None], axis=1).astype(jnp.float32)
    return lax.all_to_all(by_token, "head", split_axis=1, concat_axis=0, tiled=True)


def shards(queries, key_states, value_states, cluster_perm, block_mask):
    group_heads, shard_rows = cluster_perm.shape
    shard_blocks = shard_rows // BLOCK
    seq_count = lax.axis_size("seq")
    block_total = block_mask.shape[2]
    picks = max(1, block_total // 64)
    capacity = max(
        1, min(shard_blocks, (group_heads * picks * 8 + 5 * seq_count - 1) // (5 * seq_count))
    )
    slots = seq_count * capacity
    rows, columns = queries.shape
    group, me = lax.axis_index("head"), lax.axis_index("seq")
    ids = jnp.stack([group, me]).astype(jnp.int32)
    vmem = pl.BlockSpec(memory_space=pltpu.VMEM)
    smem = pl.BlockSpec(memory_space=pltpu.SMEM)
    anywhere = pl.BlockSpec(memory_space=pl.ANY)
    struct = jax.ShapeDtypeStruct
    bf16, i32 = jnp.bfloat16, jnp.int32

    requests, positions = pl.pallas_call(
        functools.partial(routing_kernel, shard_blocks, capacity, picks),
        out_shape=(struct((seq_count, 1, 128), i32), struct((group_heads, 128), i32)),
        in_specs=[vmem], out_specs=(vmem, vmem), name="routing",
    )(block_mask)

    dma = pltpu.SemaphoreType.DMA
    perm_blocks = cluster_perm.reshape(group_heads * shard_blocks, 1, BLOCK)
    kv_half = pltpu.VMEM((2, group_heads, rows, HEAD_DIM), bf16)
    got, pos_far = pl.pallas_call(
        functools.partial(exchange_kernel, seq_count, capacity),
        out_shape=(
            struct((2, seq_count, capacity, BLOCK, 2 * HEAD_DIM), bf16),
            struct((group_heads, 128), i32),
        ),
        in_specs=[anywhere, anywhere, vmem, vmem, vmem],
        out_specs=(anywhere, vmem),
        scratch_shapes=[
            kv_half, kv_half,
            pltpu.VMEM((seq_count, 1, 128), i32),
            pltpu.SMEM((seq_count, 1, 128), i32),
            pltpu.VMEM((seq_count, capacity, BLOCK, 2 * HEAD_DIM), bf16),
            pltpu.VMEM((8 * -(-capacity // 8), 128), i32),
            dma((2 * group_heads,)), dma((2 * group_heads,)), dma((2 * group_heads,)),
            dma((seq_count,)), dma((seq_count,)), dma((5,)),
        ] + [dma((seq_count,)) for _ in range(4)],
        compiler_params=pltpu.CompilerParams(collective_id=0, has_side_effects=True),
        name="exchange",
    )(key_states, value_states, perm_blocks, requests, positions)
    got = got.reshape(2 * slots, BLOCK, 2 * HEAD_DIM)

    masked = picks > 1
    total_heads = columns // HEAD_DIM
    width = 8 if total_heads % 8 == 0 else 1
    in_specs = [
        pl.BlockSpec((rows, width * HEAD_DIM), lambda i, *_: (0, i)),
        pl.BlockSpec(got.shape, lambda i, *_: (0, 0, 0)),
    ]
    operands = [queries, got]
    if masked:
        in_specs.append(pl.BlockSpec((width, rows, picks), lambda i, *_: (i, 0, 0)))
        operands.append(token_allow(cluster_perm, block_mask, picks, me, shard_rows))
    return pl.pallas_call(
        functools.partial(attend_kernel, group_heads, picks, slots, masked),
        out_shape=struct((rows, columns), bf16),
        grid_spec=pltpu.PrefetchScalarGridSpec(
            num_scalar_prefetch=3,
            grid=(total_heads // width,),
            in_specs=in_specs,
            out_specs=pl.BlockSpec((rows, width * HEAD_DIM), lambda i, *_: (0, i)),
        ),
        compiler_params=pltpu.CompilerParams(vmem_limit_bytes=56 * 1024 * 1024),
        name="attend",
    )(ids, positions, pos_far, *operands)


def solution(mesh):
    rows = P(("seq", "head"), None)
    placed = (rows, rows, rows, P("head", "seq"), P("head", "seq", None))
    return jax.shard_map(shards, mesh=mesh, in_specs=placed, out_specs=rows, check_vma=False)
```

```python
import functools
import math

import jax
import jax.numpy as jnp
from jax import lax
from jax.experimental import pallas as pl
from jax.experimental.pallas import tpu as pltpu
from jax.sharding import PartitionSpec as P

HEAD_DIM = 128
BLOCK = 128
MESH = pl.DeviceIdType.MESH
HIGHEST = lax.Precision.HIGHEST


def iota(shape, dim):
    return lax.broadcasted_iota(jnp.int32, shape, dim)


def partner_of(me, step, count):
    if count & (count - 1):
        raise ValueError("seq size")
    peer = 0
    bit = 1
    while bit < count:
        peer = peer + bit * (((me // bit) + (step // bit)) % 2)
        bit *= 2
    return peer


def route(shard_blocks, capacity, picks, mask_ref, req_ref, pos_ref):
    heads, _, blocks = mask_ref.shape
    seq_count = blocks // shard_blocks
    needed = jnp.max(mask_ref[...], axis=1).astype(jnp.float32)
    row, col = iota((blocks, blocks), 0), iota((blocks, blocks), 1)
    same = (row // shard_blocks) == (col // shard_blocks)
    dot = functools.partial(jnp.dot, precision=HIGHEST, preferred_element_type=jnp.float32)
    ones = lambda flag: flag.astype(jnp.float32)
    by_owner = dot(needed, ones(same))
    before_in_owner = dot(needed, ones(same & (row < col)))
    before_all = dot(needed, ones(row < col))
    lower = ones(iota((heads, heads), 1) < iota((heads, heads), 0))
    rank = dot(lower, by_owner) + before_in_owner
    head_ids, block_ids = iota((heads, blocks), 0), iota((heads, blocks), 1)
    pair = (block_ids % shard_blocks * heads + head_ids).astype(jnp.float32)
    slot_row = iota((128, blocks), 0)
    sums = jnp.zeros((128, blocks), jnp.float32)
    for c in range(capacity):
        hit = jnp.where((rank == c) & (needed > 0.5), pair, 0.0)
        sums = jnp.where(slot_row == 2 * c, jnp.sum(hit, axis=0, keepdims=True), sums)
        hit = jnp.where((rank == c) & (needed > 0.5), head_ids.astype(jnp.float32), 0.0)
        sums = jnp.where(slot_row == 2 * c + 1, jnp.sum(hit, axis=0, keepdims=True), sums)
    owner_t = ones(iota((seq_count, blocks), 1) // shard_blocks == iota((seq_count, blocks), 0))
    asked = lax.dot_general(
        owner_t, sums, (((1,), (1,)), ((), ())), precision=HIGHEST,
        preferred_element_type=jnp.float32,
    )
    req_ref[...] = (asked + 0.5).astype(jnp.int32)[:, None, :]
    position = (block_ids // shard_blocks * capacity).astype(jnp.float32) + rank
    lane = iota((heads, 128), 1)
    table = jnp.zeros((heads, 128), jnp.float32)
    for p in range(picks):
        here = jnp.where((before_all == p) & (needed > 0.5), position, 0.0)
        table = jnp.where(lane == p, jnp.sum(here, axis=1, keepdims=True), table)
    pos_ref[...] = (table + 0.5).astype(jnp.int32)


def order(i, me, count):
    top, next_bit = (me // (count // 2)) % 2, (me // (count // 4)) % 2
    end = (top + next_bit + 1) % 2
    return end * (1 + (i + count // 4 - 1) % (count - 1)) + (1 - end) * (count - 1 - i)


def exchange_kernel(
    seq_count, capacity, shard_blocks, picks,
    key_ref, value_ref, perm_ref, mask_ref, got_ref, pos_ref, pos_out,
    near_key, near_value, far_key, far_value, req_ref, asked_ref, asked, send_ref, rows_ref, blocks_ref,
    load_sem, swap_send, swap_recv, req_send, req_recv, misc_sem,
    sends, recvs, relay_send, relay_recv,
):
    group, me = lax.axis_index("head"), lax.axis_index("seq")
    other = 1 - group
    near_kv, far_kv = (near_key, near_value), (far_key, far_value)
    heads, rows = near_key.shape[:2]
    barrier = pltpu.get_barrier_semaphore()
    pl.semaphore_signal(barrier, inc=1, device_id={"head": other}, device_id_type=MESH)

    def greet(step, carry):
        pl.semaphore_signal(
            barrier, inc=1, device_id={"seq": partner_of(me, step, seq_count)}, device_id_type=MESH
        )
        return carry

    lax.fori_loop(1, seq_count, greet, 0)
    loads = []
    for number, src in enumerate((key_ref, value_ref)):
        for head in range(heads):
            start_at = pl.multiple_of((group * heads + head) * HEAD_DIM, HEAD_DIM)
            loads.append(
                pltpu.make_async_copy(
                    src.at[:, pl.ds(start_at, HEAD_DIM)], near_kv[number].at[head],
                    load_sem.at[number * heads + head],
                )
            )
    for copy in loads:
        copy.start()
    pl.semaphore_wait(barrier, seq_count)

    swaps = []
    for number, src in enumerate((key_ref, value_ref)):
        for head in range(heads):
            start_at = pl.multiple_of((other * heads + head) * HEAD_DIM, HEAD_DIM)
            at = number * heads + head
            swaps.append(
                pltpu.make_async_remote_copy(
                    src_ref=src.at[:, pl.ds(start_at, HEAD_DIM)], dst_ref=far_kv[number].at[head],
                    send_sem=swap_send.at[at], recv_sem=swap_recv.at[at],
                    device_id={"head": other}, device_id_type=MESH,
                )
            )
    for copy in swaps:
        copy.start()
    route(shard_blocks, capacity, picks, mask_ref, req_ref, pos_ref)
    for b in range(shard_blocks):
        blocks_ref[b * heads : (b + 1) * heads] = perm_ref[:, b * BLOCK : (b + 1) * BLOCK][:, None, :]
    rows_ref[...] = jnp.zeros_like(rows_ref)

    def ask(step, landing):
        peer = partner_of(me, step, seq_count)
        return pltpu.make_async_remote_copy(
            src_ref=req_ref.at[peer], dst_ref=asked_ref.at[peer if landing else me],
            send_sem=req_send.at[step], recv_sem=req_recv.at[step],
            device_id={"seq": peer}, device_id_type=MESH,
        )

    def start_ask(step, carry):
        ask(step, False).start()
        return carry

    lax.fori_loop(1, seq_count, start_ask, 0)
    tell = pltpu.make_async_remote_copy(
        src_ref=pos_ref, dst_ref=pos_out, send_sem=misc_sem.at[0], recv_sem=misc_sem.at[1],
        device_id={"head": other}, device_id_type=MESH,
    )
    tell.start()
    keep = pltpu.make_async_copy(req_ref.at[me], asked_ref.at[me], misc_sem.at[2])
    keep.start()
    keep.wait()

    def finish_ask(step, carry):
        ask(step, True).wait()
        return carry

    lax.fori_loop(1, seq_count, finish_ask, 0)
    to_scalar = pltpu.make_async_copy(asked_ref, asked, misc_sem.at[3])
    to_scalar.start()
    to_scalar.wait()
    base = me * (2 * rows)
    token = iota((BLOCK, rows), 1)
    near = token + (base + group * rows)
    far = token + (base + other * rows)

    def gather(which, peer):
        chosen = []
        for c in range(capacity):
            pair = jnp.clip(asked[peer, 0, 2 * c], 0, heads * shard_blocks - 1)
            rows_ref[c : c + 1, :] = blocks_ref[pair]
            chosen.append(jnp.clip(asked[peer, 0, 2 * c + 1], 0, heads - 1))
        turned = rows_ref[...].T
        for c, head in enumerate(chosen):
            column = turned[:, c : c + 1]
            near_table = (column == near).astype(jnp.float32).astype(jnp.bfloat16)
            far_table = (column == far).astype(jnp.float32).astype(jnp.bfloat16)
            got = jnp.dot(near_table, near_kv[which][head], preferred_element_type=jnp.float32)
            got += jnp.dot(far_table, far_kv[which][head], preferred_element_type=jnp.float32)
            send_ref[which, peer, c] = got.astype(jnp.bfloat16)

    def deliver(which, step, landing):
        peer = partner_of(me, step, seq_count)
        return pltpu.make_async_remote_copy(
            src_ref=send_ref.at[which, peer],
            dst_ref=got_ref.at[0, which, peer if landing else me],
            send_sem=sends.at[which, step], recv_sem=recvs.at[which, step],
            device_id={"seq": peer}, device_id_type=MESH,
        )

    def relay(which, step):
        peer = partner_of(me, step, seq_count)
        return pltpu.make_async_remote_copy(
            src_ref=got_ref.at[0, which, peer], dst_ref=got_ref.at[1, which, peer],
            send_sem=relay_send.at[which, step], recv_sem=relay_recv.at[which, step],
            device_id={"head": other}, device_id_type=MESH,
        )

    for which in range(2):
        for copy in loads[which * heads : (which + 1) * heads]:
            copy.wait()
        for copy in swaps[which * heads : (which + 1) * heads]:
            copy.wait()
        gather(which, partner_of(me, order(0, me, seq_count), seq_count))

        def produce(i, carry, which=which):
            gather(which, partner_of(me, order(i, me, seq_count), seq_count))
            deliver(which, order(i - 1, me, seq_count), False).start()
            return carry

        lax.fori_loop(1, seq_count - 1, produce, 0)
        gather(which, me)
        deliver(which, order(seq_count - 2, me, seq_count), False).start()

    locals_ = []
    for which in range(2):
        mine = pltpu.make_async_copy(
            send_ref.at[which, me], got_ref.at[0, which, me], misc_sem.at[4 + which]
        )
        share = pltpu.make_async_remote_copy(
            src_ref=send_ref.at[which, me], dst_ref=got_ref.at[1, which, me],
            send_sem=relay_send.at[which, 0], recv_sem=relay_recv.at[which, 0],
            device_id={"head": other}, device_id_type=MESH,
        )
        mine.start()
        share.start()
        locals_.extend((mine, share))

    for which in range(2):

        def pass_on(i, carry, which=which):
            step = order(i, me, seq_count)
            deliver(which, step, True).wait_recv()
            relay(which, step).start()
            return carry

        lax.fori_loop(0, seq_count - 1, pass_on, 0)

    def finish(step, carry):
        for which in range(2):
            deliver(which, step, True).wait_send()
            relay(which, step).wait()
        return carry

    lax.fori_loop(1, seq_count, finish, 0)
    for copy in locals_:
        copy.wait()
    tell.wait()


def attend_kernel(heads, picks, slots, masked, pos_own, pos_far, *refs):
    if masked:
        query_ref, kv_ref, allow_ref, out_ref = refs
    else:
        query_ref, kv_ref, out_ref = refs
    group = lax.axis_index("head")
    width = query_ref.shape[1] // HEAD_DIM
    scale = 1.0 / math.sqrt(HEAD_DIM)
    slot_of, scores = [], []
    for w in range(width):
        head = pl.program_id(0) * width + w
        away = (head // heads) != group
        local = head % heads
        query = query_ref[:, w * HEAD_DIM : (w + 1) * HEAD_DIM]
        for p in range(picks):
            slot = jnp.where(away, pos_far[local, p] + 2 * slots, pos_own[local, p])
            slot_of.append(slot)
            score = lax.dot_general(
                query, kv_ref[slot], (((1,), (1,)), ((), ())),
                preferred_element_type=jnp.float32,
            ) * scale
            if masked:
                score = jnp.where(allow_ref[w, :, p : p + 1] > 0, score, -jnp.inf)
            scores.append(score)
    weights = []
    for w in range(width):
        own = scores[w * picks : (w + 1) * picks]
        top = functools.reduce(jnp.maximum, [jnp.max(s, axis=1, keepdims=True) for s in own])
        exps = [jnp.exp(s - top) for s in own]
        total = functools.reduce(jnp.add, [jnp.sum(e, axis=1, keepdims=True) for e in exps])
        inverse = 1.0 / total
        weights.extend([(e * inverse).astype(jnp.bfloat16) for e in exps])
    mixed = []
    for w in range(width):
        parts = [
            jnp.dot(
                weights[w * picks + p], kv_ref[slot_of[w * picks + p] + slots],
                preferred_element_type=jnp.float32,
            )
            for p in range(picks)
        ]
        mixed.append(functools.reduce(jnp.add, parts).astype(jnp.bfloat16))
    for w in range(width):
        out_ref[:, w * HEAD_DIM : (w + 1) * HEAD_DIM] = mixed[w]


def token_allow(cluster_perm, block_mask, picks, me, shard_rows):
    needed = jnp.max(block_mask, axis=1)
    prefix = jnp.cumsum(needed, axis=1) - needed
    chosen = (needed[:, :, None] == 1) & (prefix[:, :, None] == jnp.arange(picks)[None, None, :])
    live = jnp.einsum(
        "hqb,hbp->hqp", block_mask.astype(jnp.float32), chosen.astype(jnp.float32)
    )
    group_heads = cluster_perm.shape[0]
    local = cluster_perm - me * shard_rows
    place = jnp.zeros((group_heads, shard_rows), jnp.int32)
    place = place.at[jnp.arange(group_heads)[:, None], local].set(
        jnp.broadcast_to(jnp.arange(shard_rows, dtype=jnp.int32) // BLOCK, local.shape)
    )
    by_token = jnp.take_along_axis(live, place[:, :, None], axis=1).astype(jnp.float32)
    return lax.all_to_all(by_token, "head", split_axis=1, concat_axis=0, tiled=True)


def shards(queries, key_states, value_states, cluster_perm, block_mask):
    group_heads, shard_rows = cluster_perm.shape
    shard_blocks = shard_rows // BLOCK
    seq_count = lax.axis_size("seq")
    block_total = block_mask.shape[2]
    picks = max(1, block_total // 64)
    capacity = max(
        1, min(shard_blocks, (group_heads * picks * 8 + 5 * seq_count - 1) // (5 * seq_count))
    )
    slots = seq_count * capacity
    rows, columns = queries.shape
    me = lax.axis_index("seq")
    vmem = pl.BlockSpec(memory_space=pltpu.VMEM)
    anywhere = pl.BlockSpec(memory_space=pl.ANY)
    struct = jax.ShapeDtypeStruct
    bf16, i32 = jnp.bfloat16, jnp.int32

    dma = pltpu.SemaphoreType.DMA
    kv_half = pltpu.VMEM((group_heads, rows, HEAD_DIM), bf16)
    table = struct((group_heads, 128), i32)
    got, positions, pos_far = pl.pallas_call(
        functools.partial(exchange_kernel, seq_count, capacity, shard_blocks, picks),
        out_shape=(struct((2, 2, seq_count, capacity, BLOCK, HEAD_DIM), bf16), table, table),
        in_specs=[anywhere, anywhere, vmem, vmem],
        out_specs=(anywhere, vmem, vmem),
        scratch_shapes=[
            kv_half, kv_half, kv_half, kv_half,
            pltpu.VMEM((seq_count, 1, 128), i32),
            pltpu.VMEM((seq_count, 1, 128), i32),
            pltpu.SMEM((seq_count, 1, 128), i32),
            pltpu.VMEM((2, seq_count, capacity, BLOCK, HEAD_DIM), bf16),
            pltpu.VMEM((8 * -(-capacity // 8), 128), i32),
            pltpu.VMEM((shard_blocks * group_heads, 1, BLOCK), i32),
            dma((2 * group_heads,)), dma((2 * group_heads,)), dma((2 * group_heads,)),
            dma((seq_count,)), dma((seq_count,)), dma((6,)),
        ] + [dma((2, seq_count)) for _ in range(4)],
        compiler_params=pltpu.CompilerParams(collective_id=0, has_side_effects=True),
        name="exchange",
    )(key_states, value_states, cluster_perm, block_mask)
    got = got.reshape(4 * slots, BLOCK, HEAD_DIM)

    masked = picks > 1
    total_heads = columns // HEAD_DIM
    width = 8 if total_heads % 8 == 0 else 1
    in_specs = [
        pl.BlockSpec((rows, width * HEAD_DIM), lambda i, *_: (0, i)),
        pl.BlockSpec(got.shape, lambda i, *_: (0, 0, 0)),
    ]
    operands = [queries, got]
    if masked:
        in_specs.append(pl.BlockSpec((width, rows, picks), lambda i, *_: (i, 0, 0)))
        operands.append(token_allow(cluster_perm, block_mask, picks, me, shard_rows))
    return pl.pallas_call(
        functools.partial(attend_kernel, group_heads, picks, slots, masked),
        out_shape=struct((rows, columns), bf16),
        grid_spec=pltpu.PrefetchScalarGridSpec(
            num_scalar_prefetch=2,
            grid=(total_heads // width,),
            in_specs=in_specs,
            out_specs=pl.BlockSpec((rows, width * HEAD_DIM), lambda i, *_: (0, i)),
        ),
        compiler_params=pltpu.CompilerParams(vmem_limit_bytes=56 * 1024 * 1024),
        name="attend",
    )(positions, pos_far, *operands)


def solution(mesh):
    rows = P(("seq", "head"), None)
    placed = (rows, rows, rows, P("head", "seq"), P("head", "seq", None))
    return jax.shard_map(shards, mesh=mesh, in_specs=placed, out_specs=rows, check_vma=False)
```

```python
import functools
import math

import jax
import jax.numpy as jnp
from jax import lax
from jax.experimental import pallas as pl
from jax.experimental.pallas import tpu as pltpu
from jax.sharding import PartitionSpec as P

HEAD_DIM = 128
BLOCK = 128
MESH = pl.DeviceIdType.MESH
HIGHEST = lax.Precision.HIGHEST


def iota(shape, dim):
    return lax.broadcasted_iota(jnp.int32, shape, dim)


def partner_of(me, step, count):
    if count & (count - 1):
        raise ValueError("seq size")
    peer = 0
    bit = 1
    while bit < count:
        peer = peer + bit * (((me // bit) + (step // bit)) % 2)
        bit *= 2
    return peer


def route(shard_blocks, capacity, picks, mask_ref, req_ref, pos_ref):
    heads, _, blocks = mask_ref.shape
    seq_count = blocks // shard_blocks
    needed = jnp.max(mask_ref[...], axis=1).astype(jnp.float32)
    row, col = iota((blocks, blocks), 0), iota((blocks, blocks), 1)
    same = (row // shard_blocks) == (col // shard_blocks)
    dot = functools.partial(jnp.dot, precision=HIGHEST, preferred_element_type=jnp.float32)
    ones = lambda flag: flag.astype(jnp.float32)
    by_owner = dot(needed, ones(same))
    before_in_owner = dot(needed, ones(same & (row < col)))
    before_all = dot(needed, ones(row < col))
    lower = ones(iota((heads, heads), 1) < iota((heads, heads), 0))
    rank = dot(lower, by_owner) + before_in_owner
    head_ids, block_ids = iota((heads, blocks), 0), iota((heads, blocks), 1)
    pair = (block_ids % shard_blocks * heads + head_ids).astype(jnp.float32)
    slot_row = iota((128, blocks), 0)
    sums = jnp.zeros((128, blocks), jnp.float32)
    for c in range(capacity):
        hit = jnp.where((rank == c) & (needed > 0.5), pair, 0.0)
        sums = jnp.where(slot_row == 2 * c, jnp.sum(hit, axis=0, keepdims=True), sums)
        hit = jnp.where((rank == c) & (needed > 0.5), head_ids.astype(jnp.float32), 0.0)
        sums = jnp.where(slot_row == 2 * c + 1, jnp.sum(hit, axis=0, keepdims=True), sums)
    owner_t = ones(iota((seq_count, blocks), 1) // shard_blocks == iota((seq_count, blocks), 0))
    asked = lax.dot_general(
        owner_t, sums, (((1,), (1,)), ((), ())), precision=HIGHEST,
        preferred_element_type=jnp.float32,
    )
    req_ref[...] = (asked + 0.5).astype(jnp.int32)[:, None, :]
    position = (block_ids // shard_blocks * capacity).astype(jnp.float32) + rank
    lane = iota((heads, 128), 1)
    table = jnp.zeros((heads, 128), jnp.float32)
    for p in range(picks):
        here = jnp.where((before_all == p) & (needed > 0.5), position, 0.0)
        table = jnp.where(lane == p, jnp.sum(here, axis=1, keepdims=True), table)
    pos_ref[...] = (table + 0.5).astype(jnp.int32)


def order(i, me, count):
    top, next_bit = (me // (count // 2)) % 2, (me // (count // 4)) % 2
    end = (top + next_bit + 1) % 2
    return end * (1 + (i + count // 4 - 1) % (count - 1)) + (1 - end) * (count - 1 - i)


def exchange_kernel(
    seq_count, capacity, shard_blocks, picks,
    key_ref, value_ref, query_ref, perm_ref, mask_ref, got_ref, pos_ref, pos_out, query_out,
    near_key, near_value, far_key, far_value, req_ref, asked_ref, asked, send_ref, rows_ref, blocks_ref,
    load_sem, swap_send, swap_recv, req_send, req_recv, misc_sem,
    sends, recvs, relay_send, relay_recv,
):
    group, me = lax.axis_index("head"), lax.axis_index("seq")
    other = 1 - group
    near_kv, far_kv = (near_key, near_value), (far_key, far_value)
    heads, rows = near_key.shape[:2]
    barrier = pltpu.get_barrier_semaphore()
    pl.semaphore_signal(barrier, inc=1, device_id={"head": other}, device_id_type=MESH)

    def greet(step, carry):
        pl.semaphore_signal(
            barrier, inc=1, device_id={"seq": partner_of(me, step, seq_count)}, device_id_type=MESH
        )
        return carry

    lax.fori_loop(1, seq_count, greet, 0)
    loads = []
    for number, src in enumerate((key_ref, value_ref)):
        for head in range(heads):
            start_at = pl.multiple_of((group * heads + head) * HEAD_DIM, HEAD_DIM)
            loads.append(
                pltpu.make_async_copy(
                    src.at[:, pl.ds(start_at, HEAD_DIM)], near_kv[number].at[head],
                    load_sem.at[number * heads + head],
                )
            )
    for copy in loads:
        copy.start()
    pl.semaphore_wait(barrier, seq_count)

    swaps = []
    for number, src in enumerate((key_ref, value_ref)):
        for head in range(heads):
            start_at = pl.multiple_of((other * heads + head) * HEAD_DIM, HEAD_DIM)
            at = number * heads + head
            swaps.append(
                pltpu.make_async_remote_copy(
                    src_ref=src.at[:, pl.ds(start_at, HEAD_DIM)], dst_ref=far_kv[number].at[head],
                    send_sem=swap_send.at[at], recv_sem=swap_recv.at[at],
                    device_id={"head": other}, device_id_type=MESH,
                )
            )
    for copy in swaps:
        copy.start()
    route(shard_blocks, capacity, picks, mask_ref, req_ref, pos_ref)
    for b in range(shard_blocks):
        blocks_ref[b * heads : (b + 1) * heads] = perm_ref[:, b * BLOCK : (b + 1) * BLOCK][:, None, :]
    rows_ref[...] = jnp.zeros_like(rows_ref)

    def ask(step, landing):
        peer = partner_of(me, step, seq_count)
        return pltpu.make_async_remote_copy(
            src_ref=req_ref.at[peer], dst_ref=asked_ref.at[peer if landing else me],
            send_sem=req_send.at[step], recv_sem=req_recv.at[step],
            device_id={"seq": peer}, device_id_type=MESH,
        )

    def start_ask(step, carry):
        ask(step, False).start()
        return carry

    lax.fori_loop(1, seq_count, start_ask, 0)
    tell = pltpu.make_async_remote_copy(
        src_ref=pos_ref, dst_ref=pos_out, send_sem=misc_sem.at[0], recv_sem=misc_sem.at[1],
        device_id={"head": other}, device_id_type=MESH,
    )
    tell.start()
    stay = pltpu.make_async_copy(query_ref, query_out, misc_sem.at[6])
    stay.start()
    keep = pltpu.make_async_copy(req_ref.at[me], asked_ref.at[me], misc_sem.at[2])
    keep.start()
    keep.wait()

    def finish_ask(step, carry):
        ask(step, True).wait()
        return carry

    lax.fori_loop(1, seq_count, finish_ask, 0)
    to_scalar = pltpu.make_async_copy(asked_ref, asked, misc_sem.at[3])
    to_scalar.start()
    to_scalar.wait()
    base = me * (2 * rows)
    token = iota((BLOCK, rows), 1)
    near = token + (base + group * rows)
    far = token + (base + other * rows)

    def gather(which, peer):
        chosen = []
        for c in range(capacity):
            pair = jnp.clip(asked[peer, 0, 2 * c], 0, heads * shard_blocks - 1)
            rows_ref[c : c + 1, :] = blocks_ref[pair]
            chosen.append(jnp.clip(asked[peer, 0, 2 * c + 1], 0, heads - 1))
        turned = rows_ref[...].T
        for c, head in enumerate(chosen):
            column = turned[:, c : c + 1]
            near_table = (column == near).astype(jnp.float32).astype(jnp.bfloat16)
            far_table = (column == far).astype(jnp.float32).astype(jnp.bfloat16)
            got = jnp.dot(near_table, near_kv[which][head], preferred_element_type=jnp.float32)
            got += jnp.dot(far_table, far_kv[which][head], preferred_element_type=jnp.float32)
            send_ref[which, peer, c] = got.astype(jnp.bfloat16)

    def deliver(which, step, landing):
        peer = partner_of(me, step, seq_count)
        return pltpu.make_async_remote_copy(
            src_ref=send_ref.at[which, peer],
            dst_ref=got_ref.at[0, which, peer if landing else me],
            send_sem=sends.at[which, step], recv_sem=recvs.at[which, step],
            device_id={"seq": peer}, device_id_type=MESH,
        )

    def relay(which, step):
        peer = partner_of(me, step, seq_count)
        return pltpu.make_async_remote_copy(
            src_ref=got_ref.at[0, which, peer], dst_ref=got_ref.at[1, which, peer],
            send_sem=relay_send.at[which, step], recv_sem=relay_recv.at[which, step],
            device_id={"head": other}, device_id_type=MESH,
        )

    for which in range(2):
        for copy in loads[which * heads : (which + 1) * heads]:
            copy.wait()
        for copy in swaps[which * heads : (which + 1) * heads]:
            copy.wait()
        gather(which, partner_of(me, order(0, me, seq_count), seq_count))

        def produce(i, carry, which=which):
            gather(which, partner_of(me, order(i, me, seq_count), seq_count))
            deliver(which, order(i - 1, me, seq_count), False).start()
            return carry

        lax.fori_loop(1, seq_count - 1, produce, 0)
        gather(which, me)
        deliver(which, order(seq_count - 2, me, seq_count), False).start()

    locals_ = []
    for which in range(2):
        mine = pltpu.make_async_copy(
            send_ref.at[which, me], got_ref.at[0, which, me], misc_sem.at[4 + which]
        )
        share = pltpu.make_async_remote_copy(
            src_ref=send_ref.at[which, me], dst_ref=got_ref.at[1, which, me],
            send_sem=relay_send.at[which, 0], recv_sem=relay_recv.at[which, 0],
            device_id={"head": other}, device_id_type=MESH,
        )
        mine.start()
        share.start()
        locals_.extend((mine, share))

    for which in range(2):

        def pass_on(i, carry, which=which):
            step = order(i, me, seq_count)
            deliver(which, step, True).wait_recv()
            relay(which, step).start()
            return carry

        lax.fori_loop(0, seq_count - 1, pass_on, 0)

    def finish(step, carry):
        for which in range(2):
            deliver(which, step, True).wait_send()
            relay(which, step).wait()
        return carry

    lax.fori_loop(1, seq_count, finish, 0)
    for copy in locals_:
        copy.wait()
    tell.wait()
    stay.wait()


def attend_kernel(heads, picks, width, capacity, masked, pos_own, pos_far, *refs):
    if masked:
        query_ref, kv_ref, allow_ref, out_ref, stage, sems = refs
    else:
        query_ref, kv_ref, out_ref, stage, sems = refs
    group = lax.axis_index("head")
    scale = math.log2(math.e) / math.sqrt(HEAD_DIM)
    ones = jnp.ones((BLOCK, HEAD_DIM), jnp.bfloat16)
    span = width * HEAD_DIM
    batches = query_ref.shape[1] // span

    def put(batch, buffer):
        return pltpu.make_async_copy(
            stage.at[buffer],
            out_ref.at[:, pl.ds(pl.multiple_of(batch * span, span), span)],
            sems.at[buffer],
        )

    def one(batch, carry):
        where_, scores = [], []
        for w in range(width):
            head = batch * width + w
            away = (head // heads) != group
            local = head % heads
            query = query_ref[:, pl.ds(pl.multiple_of(head * HEAD_DIM, HEAD_DIM), HEAD_DIM)]
            for p in range(picks):
                slot = jnp.where(away, pos_far[local, p], pos_own[local, p])
                spot = (slot // capacity, slot % capacity)
                rel = away.astype(jnp.int32)
                where_.append((rel, spot))
                score = lax.dot_general(
                    query, kv_ref[rel, 0, spot[0], spot[1]], (((1,), (1,)), ((), ())),
                    preferred_element_type=jnp.float32,
                )
                if masked:
                    score = jnp.where(allow_ref[head, :, p : p + 1] > 0, score, -jnp.inf)
                scores.append(score)
        weights = []
        for w in range(width):
            own = scores[w * picks : (w + 1) * picks]
            top = jnp.max(functools.reduce(jnp.maximum, own), axis=1, keepdims=True)
            weights.extend([jnp.exp2((s - top) * scale).astype(jnp.bfloat16) for s in own])
        buffer = batch % 2

        @pl.when(batch >= 2)
        def _():
            put(batch - 2, buffer).wait()

        for w in range(width):
            parts = []
            for p in range(picks):
                rel, spot = where_[w * picks + p]
                parts.append(
                    jnp.dot(
                        weights[w * picks + p],
                        jnp.concatenate([kv_ref[rel, 1, spot[0], spot[1]], ones], axis=1),
                        preferred_element_type=jnp.float32,
                    )
                )
            mixed = functools.reduce(jnp.add, parts)
            stage[buffer, :, w * HEAD_DIM : (w + 1) * HEAD_DIM] = (
                mixed[:, :HEAD_DIM] / mixed[:, HEAD_DIM:]
            ).astype(jnp.bfloat16)
        put(batch, buffer).start()
        return carry

    lax.fori_loop(0, batches, one, 0)
    for batch in range(max(0, batches - 2), batches):
        put(batch, batch % 2).wait()


def token_allow(cluster_perm, block_mask, picks, me, shard_rows):
    needed = jnp.max(block_mask, axis=1)
    prefix = jnp.cumsum(needed, axis=1) - needed
    chosen = (needed[:, :, None] == 1) & (prefix[:, :, None] == jnp.arange(picks)[None, None, :])
    live = jnp.einsum(
        "hqb,hbp->hqp", block_mask.astype(jnp.float32), chosen.astype(jnp.float32)
    )
    group_heads = cluster_perm.shape[0]
    local = cluster_perm - me * shard_rows
    place = jnp.zeros((group_heads, shard_rows), jnp.int32)
    place = place.at[jnp.arange(group_heads)[:, None], local].set(
        jnp.broadcast_to(jnp.arange(shard_rows, dtype=jnp.int32) // BLOCK, local.shape)
    )
    by_token = jnp.take_along_axis(live, place[:, :, None], axis=1).astype(jnp.float32)
    return lax.all_to_all(by_token, "head", split_axis=1, concat_axis=0, tiled=True)


def shards(queries, key_states, value_states, cluster_perm, block_mask):
    group_heads, shard_rows = cluster_perm.shape
    shard_blocks = shard_rows // BLOCK
    seq_count = lax.axis_size("seq")
    block_total = block_mask.shape[2]
    picks = max(1, block_total // 64)
    capacity = max(
        1, min(shard_blocks, (group_heads * picks * 8 + 5 * seq_count - 1) // (5 * seq_count))
    )
    rows, columns = queries.shape
    me = lax.axis_index("seq")
    vmem = pl.BlockSpec(memory_space=pltpu.VMEM)
    anywhere = pl.BlockSpec(memory_space=pltpu.HBM)
    struct = jax.ShapeDtypeStruct
    bf16, i32 = jnp.bfloat16, jnp.int32

    dma = pltpu.SemaphoreType.DMA
    kv_half = pltpu.VMEM((group_heads, rows, HEAD_DIM), bf16)
    table = struct((group_heads, 128), i32)
    resident = 2 * (4 * seq_count * capacity * BLOCK * HEAD_DIM + rows * columns)
    grant = 67043328 - resident - 256 * 1024
    got, positions, pos_far, near_queries = pl.pallas_call(
        functools.partial(exchange_kernel, seq_count, capacity, shard_blocks, picks),
        out_shape=(
            pltpu.VMEM((2, 2, seq_count, capacity, BLOCK, HEAD_DIM), bf16), table, table,
            pltpu.VMEM((rows, columns), bf16),
        ),
        in_specs=[anywhere, anywhere, anywhere, vmem, vmem],
        out_specs=(vmem, vmem, vmem, vmem),
        scratch_shapes=[
            kv_half, kv_half, kv_half, kv_half,
            pltpu.VMEM((seq_count, 1, 128), i32),
            pltpu.VMEM((seq_count, 1, 128), i32),
            pltpu.SMEM((seq_count, 1, 128), i32),
            pltpu.VMEM((2, seq_count, capacity, BLOCK, HEAD_DIM), bf16),
            pltpu.VMEM((8 * -(-capacity // 8), 128), i32),
            pltpu.VMEM((shard_blocks * group_heads, 1, BLOCK), i32),
            dma((2 * group_heads,)), dma((2 * group_heads,)), dma((2 * group_heads,)),
            dma((seq_count,)), dma((seq_count,)), dma((7,)),
        ] + [dma((2, seq_count)) for _ in range(4)],
        compiler_params=pltpu.CompilerParams(
            collective_id=0, has_side_effects=True, vmem_limit_bytes=grant
        ),
        name="exchange",
    )(key_states, value_states, queries, cluster_perm, block_mask)

    masked = picks > 1
    total_heads = columns // HEAD_DIM
    width = 8 if total_heads % 8 == 0 else 1
    operands = [near_queries, got]
    if masked:
        operands.append(token_allow(cluster_perm, block_mask, picks, me, shard_rows))
    smem = pl.BlockSpec(memory_space=pltpu.SMEM)
    return pl.pallas_call(
        functools.partial(attend_kernel, group_heads, picks, width, capacity, masked),
        out_shape=struct((rows, columns), bf16),
        in_specs=[smem, smem] + [vmem] * len(operands),
        out_specs=anywhere,
        scratch_shapes=[pltpu.VMEM((2, rows, width * HEAD_DIM), bf16), dma((2,))],
        compiler_params=pltpu.CompilerParams(vmem_limit_bytes=24 * 1024 * 1024),
        name="attend",
    )(positions, pos_far, *operands)


def solution(mesh):
    rows = P(("seq", "head"), None)
    placed = (rows, rows, rows, P("head", "seq"), P("head", "seq", None))
    return jax.shard_map(shards, mesh=mesh, in_specs=placed, out_specs=rows, check_vma=False)
```
